32 devices in a mesh: ctx: 8 (over z, y), fsdp: 4 (over x, core).
Axes of the slice: x: 2, y: 2, z: 4, core: 2. Of those that a mesh axis runs over, the one named last changes fastest.
Arguments:
- tokens: bfloat16 [4, 2048, 1024], P('fsdp', 'ctx'), may hold values from -6 to 6
- cotangent: bfloat16 [4, 2048, 1024], P('fsdp', 'ctx'), may hold values from -6 to 6
- block_order: int32 [4, 16], P('fsdp'), may hold values from 0 to 15, each once within a row
- w_qkv: bfloat16 [1024, 2048], P(('ctx', 'fsdp')), may hold values from -0.1875 to 0.1875
- w_out: bfloat16 [1024, 1024], P(None, ('ctx', 'fsdp')), may hold values from -3.5 to 3.5
- w_gate: bfloat16 [1024, 4608], P(('ctx', 'fsdp')), may hold values from -0.1875 to 0.1875
- w_up: bfloat16 [1024, 4608], P(('ctx', 'fsdp')), may hold values from -0.1875 to 0.1875
- w_down: bfloat16 [4608, 1024], P(None, ('ctx', 'fsdp')), may hold values from -0.09375 to 0.09375
- attn_gain: float32 [1024], replicated, may hold values from 0.1 to 1.9
- ffn_gain: float32 [1024], replicated, may hold values from 0.1 to 1.9
- query_gain: float32 [64], replicated, may hold values from 0.1 to 1.9
- key_gain: float32 [64], replicated, may hold values from 0.1 to 1.9
Outputs:
- block_out: bfloat16 [4, 2048, 1024], P('fsdp', 'ctx')
- input_grad: bfloat16 [4, 2048, 1024], P('fsdp', 'ctx')
- grad_qkv: float32 [1024, 2048], P(('ctx', 'fsdp'))
- grad_out: float32 [1024, 1024], P(None, ('ctx', 'fsdp'))
- grad_gate: float32 [1024, 4608], P(('ctx', 'fsdp'))
- grad_up: float32 [1024, 4608], P(('ctx', 'fsdp'))
- grad_down: float32 [4608, 1024], P(None, ('ctx', 'fsdp'))
- grad_attn_gain: float32 [1024], replicated
- grad_ffn_gain: float32 [1024], replicated
- grad_query_gain: float32 [64], replicated
- grad_key_gain: float32 [64], replicated
The draws below stay inside these ranges and needn't reach their ends.
Inputs may be any that keep to these rules, and one draw needn't show every extreme that they name: Each row of block_order is a permutation: it names every block 0 to 15 exactly once, in no fixed pattern.
All inputs are finite; a program needn't handle non-finite values.
Results may differ from the reference program's by a relative error of at most 0.017.
Values may be sent and summed in bfloat16 or wider, within the bound.
A program may use at most 256 MiB of HBM per device.

```python
import jax
import jax.numpy as jnp
from jax import lax

D = 1024
HEADS = 16
KV_HEADS = 8
HD = 64
FF = 4608
KBLOCK = 512
HALF = 128
SEQ_LEN = 2048
SEQS = 4
BLOCKS = 16
QKV_W = 2048


def strengthened(values, key, source, target, parts, factor):
    owner, partner = [(jnp.arange(values.shape[axis_at]) // (values.shape[axis_at] // parts)).reshape([-1 if axis == axis_at else 1 for axis in range(values.ndim)]) for axis_at in (source, target)]
    chosen = jax.random.permutation(key, parts)[partner]
    strong = (owner == chosen) | (owner == (partner + parts // 2) % parts)
    return jnp.where(strong, factor * values, values)


def steps_of(rng, shape, split, least, top_value):
    factor_of, own = 1.0, jax.random.fold_in(rng, 6)
    for axis_at, parts in split:
        heights = jnp.exp(jax.random.uniform(jax.random.fold_in(own, axis_at), (parts,), jnp.float32, least / len(split), top_value / len(split)))
        factor_of = factor_of * jnp.repeat(heights, shape[axis_at] // parts).reshape([-1 if axis == axis_at else 1 for axis in range(len(shape))])
    return factor_of


def bell_draw(own_key, shape, spread, most, pieces=(), dtype=jnp.bfloat16):
    drawn = spread * jax.random.normal(own_key, shape, jnp.float32)
    if pieces:
        drawn = drawn * steps_of(own_key, shape, pieces, -0.22, 0.18)
    return jnp.clip(drawn, -most, most).astype(dtype)


def gaussian_with(key, dims, scale, bound, cuts, heavy, held_as=jnp.bfloat16):
    values = scale * jax.random.normal(key, dims, jnp.float32)
    if cuts:
        values = values * steps_of(key, dims, cuts, -0.22, 0.18)
    return jnp.clip(strengthened(values, jax.random.fold_in(key, 3), *heavy), -bound, bound).astype(held_as)


def setup_inputs(seed: int = 0) -> dict:
    seeds = jax.random.split(jax.random.key(seed), 13)
    return {
        "tokens": gaussian_with(seeds[0], (SEQS, SEQ_LEN, D), 1.0, 6.0, ((0, 4), (1, 8)), (1, 2, 8, 2.0)),
        "cotangent": gaussian_with(seeds[1], (SEQS, SEQ_LEN, D), 1.0, 6.0, ((0, 4), (1, 8)), (1, 2, 8, 2.0)),
        "block_order": jax.vmap(lambda own: jax.random.permutation(own, BLOCKS))(jax.random.split(seeds[2], SEQS)).reshape((SEQS, BLOCKS)).astype(jnp.int32),
        "w_qkv": bell_draw(seeds[3], (D, QKV_W), D ** -0.5, 0.1875, ((0, 32),)),
        "w_out": bell_draw(seeds[4], (HEADS * HD, D), (max(1, HEADS * HD * 6 // SEQ_LEN)) ** -0.5, 3.5, ((1, 32),)),
        "w_gate": bell_draw(seeds[5], (D, FF), D ** -0.5, 0.1875, ((0, 32),)),
        "w_up": bell_draw(seeds[6], (D, FF), D ** -0.5, 0.1875, ((0, 32),)),
        "w_down": bell_draw(seeds[7], (FF, D), FF ** -0.5, 0.09375, ((1, 32),)),
        "attn_gain": jnp.clip(1.0 + 0.18 * jax.random.normal(seeds[8], (D,), jnp.float32), 0.1, 1.9),
        "ffn_gain": jnp.clip(1.0 + 0.18 * jax.random.normal(seeds[9], (D,), jnp.float32), 0.1, 1.9),
        "query_gain": jnp.clip(1.0 + 0.18 * jax.random.normal(seeds[10], (HD,), jnp.float32), 0.1, 1.9),
        "key_gain": jnp.clip(1.0 + 0.18 * jax.random.normal(seeds[11], (HD,), jnp.float32), 0.1, 1.9),
    }


EPS = 1e-05
THETA = 1000000.0

@jax.custom_vjp
def low(v):
    return lax.optimization_barrier(v.astype(jnp.bfloat16)).astype(jnp.float32)

@jax.custom_vjp
def low_back(v):
    return v

def low_keep(v):
    return (low(v), None)

def low_pass(kept, grad):
    return (grad,)

def back_keep(v):
    return (v, None)

def back_low(kept, grad):
    return (low(grad),)
low.defvjp(low_keep, low_pass)
low_back.defvjp(back_keep, back_low)

def rms_norm(inputs, gain_row):
    return inputs * lax.rsqrt(lax.optimization_barrier(jnp.mean(inputs * inputs, axis=-1, keepdims=True)) + EPS) * gain_row

def rotary(inputs, cosines, sines):
    half_width = inputs.shape[-1] // 2
    turned = jnp.concatenate([-inputs[..., half_width:], inputs[..., :half_width]], axis=-1)
    return inputs * cosines + turned * sines

def angles(positions):
    exponent = jnp.arange(0, HD, 2).astype(jnp.float32) / HD
    inverse = jnp.power(THETA, -exponent)
    phases = positions.astype(jnp.float32)[:, None] * inverse[None, :]
    phases = jnp.concatenate([phases, phases], axis=-1)
    return (jnp.cos(phases)[:, None, :], jnp.sin(phases)[:, None, :])

def precise(left, right):
    return jnp.dot(left, right, precision=lax.Precision.HIGHEST)

def attend(queries, keys, values, positions):
    groups_per = HEADS // KV_HEADS
    scale = HD ** (-0.5)
    block_count = SEQ_LEN // KBLOCK
    query_blocks = queries.reshape(block_count, KBLOCK, KV_HEADS, groups_per, HD)
    spot_blocks = positions.reshape(block_count, KBLOCK)

    def one_block(pair):
        query_block, spot_block = pair
        scores = jnp.einsum('qngd,knd->ngqk', query_block, keys, precision=lax.Precision.HIGHEST) * scale
        scores = low_back(scores)
        allowed = spot_block[:, None] >= positions[None, :]
        scores = jnp.where(allowed[None, None], scores, -1e+30)
        top = lax.optimization_barrier(jnp.max(scores, axis=-1, keepdims=True))
        log_total = top + jnp.log(lax.optimization_barrier(jnp.sum(jnp.exp(scores - top), axis=-1, keepdims=True)))
        weights = low(jnp.exp(scores - log_total))
        mixed = jnp.einsum('ngqk,knd->qngd', weights, values, precision=lax.Precision.HIGHEST)
        return mixed.reshape(KBLOCK, HEADS * HD)
    mixed_all = lax.map(jax.checkpoint(one_block), (query_blocks, spot_blocks))
    return mixed_all.reshape(SEQ_LEN, HEADS * HD)

def forward(inputs, w_qkv, w_out, w_gate, w_up, w_down, attn_gain, ffn_gain, query_gain, key_gain, positions):
    q_width = HEADS * HD
    kv_width = KV_HEADS * HD
    normed = low(rms_norm(inputs, attn_gain))
    projected = low_back(precise(normed, w_qkv))
    query_raw = projected[:, :q_width].reshape(SEQ_LEN, HEADS, HD)
    key_raw = projected[:, q_width:q_width + kv_width].reshape(SEQ_LEN, KV_HEADS, HD)
    values = low(projected[:, q_width + kv_width:]).reshape(SEQ_LEN, KV_HEADS, HD)
    cosines, sines = angles(positions)
    queries = low(rotary(rms_norm(query_raw, query_gain), cosines, sines))
    keys = low(rotary(rms_norm(key_raw, key_gain), cosines, sines))
    queries = queries.reshape(SEQ_LEN, KV_HEADS, HEADS // KV_HEADS, HD)
    attended = low(low_back(attend(queries, keys, values, positions)))
    hidden = inputs + low_back(precise(attended, w_out))
    normed_two = low(rms_norm(hidden, ffn_gain))
    gate = low_back(precise(normed_two, w_gate))
    up_val = low_back(precise(normed_two, w_up))
    act = low(jax.nn.silu(gate) * up_val)
    return hidden + precise(act, w_down)

def reference(tokens, cotangent, block_order, w_qkv, w_out, w_gate, w_up, w_down, attn_gain, ffn_gain, query_gain, key_gain):
    params = (w_qkv.astype(jnp.float32), w_out.astype(jnp.float32), w_gate.astype(jnp.float32), w_up.astype(jnp.float32), w_down.astype(jnp.float32), attn_gain.astype(jnp.float32), ffn_gain.astype(jnp.float32), query_gain.astype(jnp.float32), key_gain.astype(jnp.float32))
    row_index = jnp.arange(SEQ_LEN).astype(jnp.int32)
    slot_of = (row_index // HALF).astype(jnp.int32)
    offsets = (row_index % HALF).astype(jnp.int32)

    def one_sequence(carry, item):
        seq_tokens, seq_cot, seq_order = item
        positions = (seq_order[slot_of] * HALF + offsets).astype(jnp.int32)

        def apply(inputs, *weights_all):
            return forward(inputs, *weights_all, positions)
        result, pull = jax.vjp(apply, seq_tokens.astype(jnp.float32), *params)
        grads = pull(seq_cot.astype(jnp.float32))
        new_carry = tuple((total + piece for total, piece in zip(carry, grads[1:])))
        return (new_carry, (result.astype(jnp.bfloat16), grads[0].astype(jnp.bfloat16)))
    start = tuple((jnp.zeros_like(item) for item in params))
    sums, (block_out, input_grad) = lax.scan(one_sequence, start, (tokens, cotangent, block_order))
    return (block_out, input_grad, sums[0], sums[1], sums[2], sums[3], sums[4], sums[5], sums[6], sums[7], sums[8])
```

```python
import jax
import jax.numpy as jnp
from jax import lax
from jax.experimental import pallas as pl
from jax.experimental.pallas import tpu as pltpu
from jax.sharding import PartitionSpec as P

HEADS = 16
KV_HEADS = 8
HD = 64
KBLOCK = 512


EPS = 1e-05
THETA = 1000000.0


def rms_norm(inputs, gain_row):
    return inputs * lax.rsqrt(jnp.mean(inputs * inputs, axis=-1, keepdims=True) + EPS) * gain_row


def rotary(inputs, cosines, sines):
    half_width = inputs.shape[-1] // 2
    turned = jnp.concatenate([-inputs[..., half_width:], inputs[..., :half_width]], axis=-1)
    return inputs * cosines + turned * sines


def angles(positions):
    exponent = jnp.arange(0, HD, 2).astype(jnp.float32) / HD
    inverse = jnp.power(THETA, -exponent)
    phases = positions.astype(jnp.float32)[:, None] * inverse[None, :]
    phases = jnp.concatenate([phases, phases], axis=-1)
    return (jnp.cos(phases)[:, None, :], jnp.sin(phases)[:, None, :])


PAIRS = KV_HEADS // 2
VMEM_LIMIT = 50 * 1024 * 1024


def forward_kernel(q_ref, kv_ref, qspot_ref, kspot_ref, out_ref, total_ref):
    query_cols = q_ref[0]
    query_spots = qspot_ref[...]

    def step(block, carry):
        mixed, total = carry
        rows = pl.ds(pl.multiple_of(block * KBLOCK, KBLOCK), KBLOCK)
        keys = kv_ref[rows, :128]
        values = kv_ref[rows, 128:]
        scores = jnp.dot(keys, query_cols, preferred_element_type=jnp.float32)
        allowed = query_spots >= kspot_ref[rows, :]
        weights = jnp.where(allowed, jnp.exp(scores), 0.0)
        total = total + jnp.sum(weights, axis=0, keepdims=True)
        mixed = mixed + lax.dot_general(
            values,
            weights.astype(jnp.bfloat16),
            (((0,), (0,)), ((), ())),
            preferred_element_type=jnp.float32,
        )
        return mixed, total

    columns = query_cols.shape[1]
    mixed, total = lax.fori_loop(
        0,
        kv_ref.shape[0] // KBLOCK,
        step,
        (jnp.zeros((128, columns), jnp.float32), jnp.zeros((1, columns), jnp.float32)),
    )
    out_ref[0] = mixed / total
    total_ref[0] = 1.0 / total


def backward_kernel(q_ref, do_ref, kv_ref, out_ref, inv_ref, qspot_ref, kspot_ref, dq_ref, dkv_ref):
    query_cols = q_ref[0]
    grad_cols = do_ref[0]
    query_spots = qspot_ref[...]
    inverse = inv_ref[0]
    diagonal = jnp.sum(grad_cols.astype(jnp.float32) * out_ref[0], axis=0, keepdims=True)
    last = (((1,), (1,)), ((), ()))

    def step(block, query_grad):
        rows = pl.ds(pl.multiple_of(block * KBLOCK, KBLOCK), KBLOCK)
        keys = kv_ref[rows, :128]
        values = kv_ref[rows, 128:]
        scores = jnp.dot(keys, query_cols, preferred_element_type=jnp.float32)
        allowed = query_spots >= kspot_ref[rows, :]
        probs = jnp.where(allowed, jnp.exp(scores), 0.0) * inverse
        prob_grad = jnp.dot(values, grad_cols, preferred_element_type=jnp.float32)
        score_low = (probs * (prob_grad - diagonal)).astype(jnp.bfloat16)
        dkv_ref[rows, :128] = lax.dot_general(
            score_low, query_cols, last, preferred_element_type=jnp.float32
        ).astype(jnp.bfloat16)
        dkv_ref[rows, 128:] = lax.dot_general(
            probs.astype(jnp.bfloat16), grad_cols, last, preferred_element_type=jnp.float32
        ).astype(jnp.bfloat16)
        return query_grad + lax.dot_general(
            keys, score_low, (((0,), (0,)), ((), ())), preferred_element_type=jnp.float32
        )

    dq_ref[0] = lax.fori_loop(
        0, kv_ref.shape[0] // KBLOCK, step, jnp.zeros(query_cols.shape, jnp.float32)
    )


def head_columns(rows_by_heads):
    tok_rows = rows_by_heads.shape[0]
    cols = rows_by_heads.reshape(tok_rows, PAIRS, 2, 2, HD).transpose(1, 4, 2, 3, 0)
    cols = cols.reshape(PAIRS, HD, 2, 2 * tok_rows)
    empty = jnp.zeros_like(cols[:, :, 0])
    top = jnp.concatenate([cols[:, :, 0], empty], axis=-1)
    low = jnp.concatenate([empty, cols[:, :, 1]], axis=-1)
    return jnp.concatenate([top, low], axis=1)


def column_heads(cols, tok_rows):
    top = cols[:, :HD, : 2 * tok_rows].reshape(PAIRS, HD, 2, tok_rows)
    low = cols[:, HD:, 2 * tok_rows :].reshape(PAIRS, HD, 2, tok_rows)
    both = jnp.stack([top, low], axis=1)
    return both.transpose(4, 0, 1, 3, 2).reshape(tok_rows, HEADS * HD)


def attend(query_cols, kv_all, query_row, key_col):
    seq_rows = kv_all.shape[0]
    columns = query_cols.shape[2]
    return pl.pallas_call(
        forward_kernel,
        grid=(PAIRS,),
        in_specs=[
            pl.BlockSpec((1, 128, columns), lambda p: (p, 0, 0)),
            pl.BlockSpec((seq_rows, 256), lambda p: (0, p)),
            pl.BlockSpec((1, columns), lambda p: (0, 0)),
            pl.BlockSpec((seq_rows, 1), lambda p: (0, 0)),
        ],
        out_specs=[
            pl.BlockSpec((1, 128, columns), lambda p: (p, 0, 0)),
            pl.BlockSpec((1, 1, columns), lambda p: (p, 0, 0)),
        ],
        out_shape=[
            jax.ShapeDtypeStruct((PAIRS, 128, columns), jnp.float32),
            jax.ShapeDtypeStruct((PAIRS, 1, columns), jnp.float32),
        ],
        compiler_params=pltpu.CompilerParams(vmem_limit_bytes=VMEM_LIMIT),
        cost_estimate=pl.CostEstimate(
            flops=4 * PAIRS * 128 * columns * seq_rows,
            bytes_accessed=12 * 1024 * 1024,
            transcendentals=PAIRS * columns * seq_rows,
        ),
    )(query_cols, kv_all, query_row, key_col)


def attend_back(query_cols, grad_cols, kv_all, mixed, inverse, query_row, key_col):
    seq_rows = kv_all.shape[0]
    columns = query_cols.shape[2]
    return pl.pallas_call(
        backward_kernel,
        grid=(PAIRS,),
        in_specs=[
            pl.BlockSpec((1, 128, columns), lambda p: (p, 0, 0)),
            pl.BlockSpec((1, 128, columns), lambda p: (p, 0, 0)),
            pl.BlockSpec((seq_rows, 256), lambda p: (0, p)),
            pl.BlockSpec((1, 128, columns), lambda p: (p, 0, 0)),
            pl.BlockSpec((1, 1, columns), lambda p: (p, 0, 0)),
            pl.BlockSpec((1, columns), lambda p: (0, 0)),
            pl.BlockSpec((seq_rows, 1), lambda p: (0, 0)),
        ],
        out_specs=[
            pl.BlockSpec((1, 128, columns), lambda p: (p, 0, 0)),
            pl.BlockSpec((seq_rows, 256), lambda p: (0, p)),
        ],
        out_shape=[
            jax.ShapeDtypeStruct((PAIRS, 128, columns), jnp.float32),
            jax.ShapeDtypeStruct((seq_rows, PAIRS * 256), jnp.bfloat16),
        ],
        compiler_params=pltpu.CompilerParams(vmem_limit_bytes=VMEM_LIMIT),
        cost_estimate=pl.CostEstimate(
            flops=10 * PAIRS * 128 * columns * seq_rows,
            bytes_accessed=20 * 1024 * 1024,
            transcendentals=PAIRS * columns * seq_rows,
        ),
    )(query_cols, grad_cols, kv_all, mixed, inverse, query_row, key_col)


def weave(left, right):
    tok_rows = left.shape[0]
    parts = [left.reshape(tok_rows, PAIRS, 128), right.reshape(tok_rows, PAIRS, 128)]
    return jnp.concatenate(parts, axis=-1).reshape(tok_rows, PAIRS * 256)


def unweave(both):
    tok_rows = both.shape[0]
    parts = both.reshape(tok_rows, PAIRS, 2, 128)
    return (
        parts[:, :, 0].reshape(tok_rows, PAIRS * 128),
        parts[:, :, 1].reshape(tok_rows, PAIRS * 128),
    )


def dot(left, right, left_dim, right_dim):
    return lax.dot_general(
        left, right, (((left_dim,), (right_dim,)), ((), ())), preferred_element_type=jnp.float32
    )


def body(
    tokens,
    cotangent,
    block_order,
    w_qkv,
    w_out,
    w_gate,
    w_up,
    w_down,
    attn_gain,
    ffn_gain,
    query_gain,
    key_gain,
):
    tok_rows = tokens.shape[1]
    model_width = tokens.shape[2]
    span_count = lax.axis_size("ctx")
    ways = lax.axis_size("fsdp")
    seq_rows = tok_rows * span_count
    half_rows = tok_rows // 2
    scale = HD ** (-0.5)
    q_width = HEADS * HD
    kv_width = KV_HEADS * HD
    own_rows = w_gate.shape[0]
    hidden_units = w_gate.shape[1]
    part = hidden_units // ways
    low = jnp.bfloat16
    slot_order = block_order.reshape(-1)
    key_spots = (
        slot_order[:, None] * half_rows + jnp.arange(half_rows, dtype=jnp.int32)[None, :]
    ).reshape(-1)
    query_spots = lax.dynamic_slice_in_dim(key_spots, lax.axis_index("ctx") * tok_rows, tok_rows)
    cosines, sines = angles(query_spots)
    key_col = key_spots[:, None]
    query_row = jnp.tile(query_spots, 4)[None, :]

    first_weights = lax.all_gather(
        jnp.concatenate([w_qkv, w_out.T], axis=1), ("ctx", "fsdp"), axis=0, tiled=True
    )
    full_qkv = first_weights[:, : w_qkv.shape[1]]
    out_t = first_weights[:, w_qkv.shape[1] :]
    ffn_own = jnp.concatenate(
        [
            w_gate.reshape(own_rows, ways, part),
            w_up.reshape(own_rows, ways, part),
            w_down.T.reshape(own_rows, ways, part),
        ],
        axis=-1,
    ).transpose(1, 0, 2)
    ffn_rows = lax.all_to_all(ffn_own, "fsdp", 0, 0, tiled=True)
    ffn_weights = lax.all_gather(
        ffn_rows.reshape(ways * own_rows, 3 * part), "ctx", axis=0, tiled=True
    )
    gate_part = ffn_weights[:, :part]
    up_part = ffn_weights[:, part : 2 * part]
    down_part = ffn_weights[:, 2 * part :]
    cot_low = cotangent.reshape(tok_rows, model_width)

    tok_f32 = tokens.reshape(tok_rows, model_width).astype(jnp.float32)
    normed, attn_pull = jax.vjp(rms_norm, tok_f32, attn_gain)
    normed_low = normed.astype(low)
    projected = jnp.dot(normed_low, full_qkv, preferred_element_type=jnp.float32)
    query_raw = projected[:, :q_width].reshape(tok_rows, HEADS, HD)
    key_raw = projected[:, q_width : q_width + kv_width].reshape(tok_rows, KV_HEADS, HD)
    value_low = projected[:, q_width + kv_width :].astype(low)

    def head_path(raw_heads, gain_row):
        return rotary(rms_norm(raw_heads, gain_row), cosines, sines)

    query_rot, query_pull = jax.vjp(head_path, query_raw, query_gain)
    key_rot, key_pull = jax.vjp(head_path, key_raw, key_gain)
    key_low = key_rot.astype(low).reshape(tok_rows, kv_width)
    kv_all = lax.all_gather(weave(key_low, value_low), "ctx", axis=0, tiled=True)
    query_cols = head_columns((query_rot.astype(low) * low(scale)).reshape(tok_rows, q_width))
    mixed, inverse = attend(query_cols, kv_all, query_row, key_col)
    attended_low = column_heads(mixed.astype(low), tok_rows)
    hidden = tok_f32 + dot(attended_low, out_t, 1, 1)
    normed_two, ffn_pull = jax.vjp(rms_norm, hidden, ffn_gain)
    cot_all = lax.all_gather(cot_low, "fsdp", axis=0, tiled=True)
    two_all = lax.all_gather(normed_two.astype(low), "fsdp", axis=0, tiled=True)

    gate_val = dot(two_all, gate_part, 1, 0)
    up_val = dot(two_all, up_part, 1, 0)

    def gated(gate_in, up_in):
        return jax.nn.silu(gate_in) * up_in

    activation, act_pull = jax.vjp(gated, gate_val, up_val)
    act_low = activation.astype(low)
    act_grad = dot(cot_all, down_part, 1, 0)
    gate_grad, up_grad = act_pull(act_grad)
    gate_low = gate_grad.astype(low)
    up_low = up_grad.astype(low)
    two_part = dot(gate_low, gate_part, 1, 1) + dot(up_low, up_part, 1, 1)
    normed_two_grad = lax.psum_scatter(
        two_part.astype(low), "fsdp", scatter_dimension=0, tiled=True
    ).astype(jnp.float32)
    block_part = dot(act_low, down_part, 1, 1)
    block_sum = lax.psum_scatter(
        block_part.astype(low), "fsdp", scatter_dimension=0, tiled=True
    ).astype(jnp.float32)
    block_out = (hidden + block_sum).astype(low)

    hidden_back, ffn_gain_grad = ffn_pull(normed_two_grad)
    hidden_grad = cot_low.astype(jnp.float32) + hidden_back
    hidden_low = hidden_grad.astype(low)
    attended_grad = dot(hidden_low, out_t, 1, 0).astype(low)
    grad_cols = head_columns(attended_grad)
    query_grad, kv_grad = attend_back(
        query_cols, grad_cols, kv_all, mixed, inverse, query_row, key_col
    )
    kv_sum = lax.psum_scatter(kv_grad, "ctx", scatter_dimension=0, tiled=True)
    key_sum, value_sum = unweave(kv_sum)

    grad_ffn = jnp.concatenate(
        [dot(two_all, gate_low, 0, 0), dot(two_all, up_low, 0, 0), dot(cot_all, act_low, 0, 0)],
        axis=1,
    ).astype(low)
    grad_ffn = lax.psum_scatter(grad_ffn, "ctx", scatter_dimension=0, tiled=True)
    grad_ffn = lax.all_to_all(
        grad_ffn.reshape(ways, own_rows, 3 * part), "fsdp", 0, 0, tiled=True
    ).transpose(1, 0, 2)
    grad_gate = grad_ffn[:, :, :part].reshape(own_rows, hidden_units).astype(jnp.float32)
    grad_up = grad_ffn[:, :, part : 2 * part].reshape(own_rows, hidden_units).astype(jnp.float32)
    grad_down = grad_ffn[:, :, 2 * part :].reshape(own_rows, hidden_units).T.astype(jnp.float32)

    query_back, query_gain_grad = query_pull(
        column_heads(query_grad * scale, tok_rows).reshape(tok_rows, HEADS, HD)
    )
    key_back, key_gain_grad = key_pull(
        key_sum.astype(jnp.float32).reshape(tok_rows, KV_HEADS, HD)
    )
    proj_low = jnp.concatenate(
        [
            query_back.reshape(tok_rows, q_width).astype(low),
            key_back.reshape(tok_rows, kv_width).astype(low),
            value_sum,
        ],
        axis=1,
    )
    grad_first = jnp.concatenate(
        [dot(normed_low, proj_low, 0, 0), dot(hidden_low, attended_low, 0, 0)], axis=1
    ).astype(low)
    grad_first = lax.psum_scatter(
        grad_first, ("ctx", "fsdp"), scatter_dimension=0, tiled=True
    ).astype(jnp.float32)
    grad_qkv = grad_first[:, : w_qkv.shape[1]]
    grad_out = grad_first[:, w_qkv.shape[1] :].T
    normed_grad = dot(proj_low, full_qkv, 1, 1)
    input_back, attn_gain_grad = attn_pull(normed_grad)
    input_grad = (hidden_grad + input_back).astype(low)
    attn_gain_grad, ffn_gain_grad, query_gain_grad, key_gain_grad = lax.psum(
        (attn_gain_grad, ffn_gain_grad, query_gain_grad, key_gain_grad), ("ctx", "fsdp")
    )
    return (
        block_out.reshape(1, tok_rows, model_width),
        input_grad.reshape(1, tok_rows, model_width),
        grad_qkv,
        grad_out,
        grad_gate,
        grad_up,
        grad_down,
        attn_gain_grad,
        ffn_gain_grad,
        query_gain_grad,
        key_gain_grad,
    )


def solution(mesh):
    placed = (
        P("fsdp", "ctx", None),
        P("fsdp", "ctx", None),
        P("fsdp", None),
        P(("ctx", "fsdp"), None),
        P(None, ("ctx", "fsdp")),
        P(("ctx", "fsdp"), None),
        P(("ctx", "fsdp"), None),
        P(None, ("ctx", "fsdp")),
        P(),
        P(),
        P(),
        P(),
    )
    return jax.shard_map(
        body,
        mesh=mesh,
        in_specs=placed,
        out_specs=(
            P("fsdp", "ctx", None),
            P("fsdp", "ctx", None),
            P(("ctx", "fsdp"), None),
            P(None, ("ctx", "fsdp")),
            P(("ctx", "fsdp"), None),
            P(("ctx", "fsdp"), None),
            P(None, ("ctx", "fsdp")),
            P(),
            P(),
            P(),
            P(),
        ),
        check_vma=False,
    )
```

```python
import functools

import jax
import jax.numpy as jnp
from jax import lax
from jax.experimental import pallas as pl
from jax.experimental.pallas import tpu as pltpu
from jax.sharding import PartitionSpec as P

HEADS = 16
KV_HEADS = 8
HD = 64
KBLOCK = 512


EPS = 1e-05
THETA = 1000000.0


def rms_norm(inputs, gain_row):
    return inputs * lax.rsqrt(jnp.mean(inputs * inputs, axis=-1, keepdims=True) + EPS) * gain_row


def rotary(inputs, cosines, sines):
    half_width = inputs.shape[-1] // 2
    turned = jnp.concatenate([-inputs[..., half_width:], inputs[..., :half_width]], axis=-1)
    return inputs * cosines + turned * sines


def angles(positions):
    exponent = jnp.arange(0, HD, 2).astype(jnp.float32) / HD
    inverse = jnp.power(THETA, -exponent)
    phases = positions.astype(jnp.float32)[:, None] * inverse[None, :]
    phases = jnp.concatenate([phases, phases], axis=-1)
    return (jnp.cos(phases)[:, None, :], jnp.sin(phases)[:, None, :])


PAIRS = KV_HEADS // 2
VMEM_LIMIT = 50 * 1024 * 1024


def key_depth(columns):
    return KBLOCK if columns <= 1024 else KBLOCK // 2


def forward_kernel(q_ref, kv_ref, qspot_ref, kspot_ref, out_ref, total_ref):
    query_cols = q_ref[0]
    width, columns = query_cols.shape
    depth = key_depth(columns)
    query_spots = qspot_ref[...]

    def step(block, carry):
        mixed, total = carry
        rows = pl.ds(pl.multiple_of(block * depth, depth), depth)
        keys = kv_ref[rows, :width]
        values = kv_ref[rows, width:]
        scores = jnp.dot(keys, query_cols, preferred_element_type=jnp.float32)
        allowed = query_spots >= kspot_ref[rows, :]
        weights = jnp.where(allowed, jnp.exp(scores), 0.0)
        total = total + jnp.sum(weights, axis=0, keepdims=True)
        mixed = mixed + lax.dot_general(
            values,
            weights.astype(jnp.bfloat16),
            (((0,), (0,)), ((), ())),
            preferred_element_type=jnp.float32,
        )
        return mixed, total

    mixed, total = lax.fori_loop(
        0,
        kv_ref.shape[0] // depth,
        step,
        (jnp.zeros((width, columns), jnp.float32), jnp.zeros((1, columns), jnp.float32)),
    )
    out_ref[0] = mixed / total
    total_ref[0] = 1.0 / total


def backward_kernel(q_ref, do_ref, kv_ref, out_ref, inv_ref, qspot_ref, kspot_ref, dq_ref, dkv_ref):
    query_cols = q_ref[0]
    width, columns = query_cols.shape
    depth = key_depth(columns)
    grad_cols = do_ref[0]
    query_spots = qspot_ref[...]
    inverse = inv_ref[0]
    diagonal = jnp.sum(grad_cols.astype(jnp.float32) * out_ref[0], axis=0, keepdims=True)
    last = (((1,), (1,)), ((), ()))

    def step(block, query_grad):
        rows = pl.ds(pl.multiple_of(block * depth, depth), depth)
        keys = kv_ref[rows, :width]
        values = kv_ref[rows, width:]
        scores = jnp.dot(keys, query_cols, preferred_element_type=jnp.float32)
        allowed = query_spots >= kspot_ref[rows, :]
        probs = jnp.where(allowed, jnp.exp(scores), 0.0) * inverse
        prob_grad = jnp.dot(values, grad_cols, preferred_element_type=jnp.float32)
        score_low = (probs * (prob_grad - diagonal)).astype(jnp.bfloat16)
        dkv_ref[rows, :width] = lax.dot_general(
            score_low, query_cols, last, preferred_element_type=jnp.float32
        ).astype(jnp.bfloat16)
        dkv_ref[rows, width:] = lax.dot_general(
            probs.astype(jnp.bfloat16), grad_cols, last, preferred_element_type=jnp.float32
        ).astype(jnp.bfloat16)
        return query_grad + lax.dot_general(
            keys, score_low, (((0,), (0,)), ((), ())), preferred_element_type=jnp.float32
        )

    dq_ref[0] = lax.fori_loop(
        0, kv_ref.shape[0] // depth, step, jnp.zeros(query_cols.shape, jnp.float32)
    )


def head_columns(rows_by_heads):
    tok_rows = rows_by_heads.shape[0]
    cols = rows_by_heads.reshape(tok_rows, PAIRS, 2, 2, HD).transpose(1, 4, 2, 3, 0)
    cols = cols.reshape(PAIRS, HD, 2, 2 * tok_rows)
    empty = jnp.zeros_like(cols[:, :, 0])
    top = jnp.concatenate([cols[:, :, 0], empty], axis=-1)
    low = jnp.concatenate([empty, cols[:, :, 1]], axis=-1)
    return jnp.concatenate([top, low], axis=1)


def column_heads(cols, tok_rows):
    top = cols[:, :HD, : 2 * tok_rows].reshape(PAIRS, HD, 2, tok_rows)
    low = cols[:, HD:, 2 * tok_rows :].reshape(PAIRS, HD, 2, tok_rows)
    both = jnp.stack([top, low], axis=1)
    return both.transpose(4, 0, 1, 3, 2).reshape(tok_rows, HEADS * HD)


def attend(query_cols, kv_all, query_row, key_col):
    seq_rows = kv_all.shape[0]
    groups, width, columns = query_cols.shape
    return pl.pallas_call(
        forward_kernel,
        grid=(groups,),
        in_specs=[
            pl.BlockSpec((1, width, columns), lambda p: (p, 0, 0)),
            pl.BlockSpec((seq_rows, 2 * width), lambda p: (0, p)),
            pl.BlockSpec((1, columns), lambda p: (0, 0)),
            pl.BlockSpec((seq_rows, 1), lambda p: (0, 0)),
        ],
        out_specs=[
            pl.BlockSpec((1, width, columns), lambda p: (p, 0, 0)),
            pl.BlockSpec((1, 1, columns), lambda p: (p, 0, 0)),
        ],
        out_shape=[
            jax.ShapeDtypeStruct((groups, width, columns), jnp.float32),
            jax.ShapeDtypeStruct((groups, 1, columns), jnp.float32),
        ],
        compiler_params=pltpu.CompilerParams(vmem_limit_bytes=VMEM_LIMIT),
        cost_estimate=pl.CostEstimate(
            flops=4 * groups * width * columns * seq_rows,
            bytes_accessed=12 * 1024 * 1024,
            transcendentals=groups * columns * seq_rows,
        ),
    )(query_cols, kv_all, query_row, key_col)


def attend_back(query_cols, grad_cols, kv_all, mixed, inverse, query_row, key_col):
    seq_rows = kv_all.shape[0]
    groups, width, columns = query_cols.shape
    return pl.pallas_call(
        backward_kernel,
        grid=(groups,),
        in_specs=[
            pl.BlockSpec((1, width, columns), lambda p: (p, 0, 0)),
            pl.BlockSpec((1, width, columns), lambda p: (p, 0, 0)),
            pl.BlockSpec((seq_rows, 2 * width), lambda p: (0, p)),
            pl.BlockSpec((1, width, columns), lambda p: (p, 0, 0)),
            pl.BlockSpec((1, 1, columns), lambda p: (p, 0, 0)),
            pl.BlockSpec((1, columns), lambda p: (0, 0)),
            pl.BlockSpec((seq_rows, 1), lambda p: (0, 0)),
        ],
        out_specs=[
            pl.BlockSpec((1, width, columns), lambda p: (p, 0, 0)),
            pl.BlockSpec((seq_rows, 2 * width), lambda p: (0, p)),
        ],
        out_shape=[
            jax.ShapeDtypeStruct((groups, width, columns), jnp.float32),
            jax.ShapeDtypeStruct((seq_rows, groups * 2 * width), jnp.bfloat16),
        ],
        compiler_params=pltpu.CompilerParams(vmem_limit_bytes=VMEM_LIMIT),
        cost_estimate=pl.CostEstimate(
            flops=10 * groups * width * columns * seq_rows,
            bytes_accessed=20 * 1024 * 1024,
            transcendentals=groups * columns * seq_rows,
        ),
    )(query_cols, grad_cols, kv_all, mixed, inverse, query_row, key_col)


def exchange_kernel(axis, count, spread, src, dst, own_sem, send_sems, recv_sems):
    me = lax.axis_index(axis)
    barrier = pltpu.get_barrier_semaphore()
    for step in range(1, count):
        pl.semaphore_signal(
            barrier,
            inc=1,
            device_id={axis: lax.rem(me + step, count)},
            device_id_type=pl.DeviceIdType.MESH,
        )
    pl.semaphore_wait(barrier, count - 1)
    copies = []
    for step in range(1, count):
        peer = lax.rem(me + step, count)
        copies.append(
            pltpu.make_async_remote_copy(
                src_ref=src if spread else src.at[peer],
                dst_ref=dst.at[me],
                send_sem=send_sems.at[step - 1],
                recv_sem=recv_sems.at[step - 1],
                device_id={axis: peer},
                device_id_type=pl.DeviceIdType.MESH,
            )
        )
    for copy in copies:
        copy.start()
    own = pltpu.make_async_copy(src if spread else src.at[me], dst.at[me], own_sem)
    own.start()
    own.wait()
    for copy in copies:
        copy.wait()


def exchange(block, axis, number, spread=False):
    count = lax.axis_size(axis)
    shape = (count,) + (block.shape if spread else block.shape[1:])
    return pl.pallas_call(
        functools.partial(exchange_kernel, axis, count, spread),
        in_specs=[pl.BlockSpec(memory_space=pl.ANY)],
        out_specs=pl.BlockSpec(memory_space=pl.ANY),
        out_shape=jax.ShapeDtypeStruct(shape, block.dtype),
        scratch_shapes=[
            pltpu.SemaphoreType.DMA,
            pltpu.SemaphoreType.DMA((count - 1,)),
            pltpu.SemaphoreType.DMA((count - 1,)),
        ],
        compiler_params=pltpu.CompilerParams(collective_id=number, has_side_effects=True),
        cost_estimate=pl.CostEstimate(flops=0, bytes_accessed=40_000_000, transcendentals=0),
    )(block)


def split_heads(cols, spans):
    total = cols.shape[1] // 2
    return cols.reshape(HD, 2, total).transpose(2, 1, 0).reshape(spans, total // spans, 2 * HD)


def join_heads(rows):
    total = rows.shape[0]
    return rows.reshape(total, 2, HD).transpose(2, 1, 0).reshape(1, HD, 2 * total)


def weave(left, right):
    tok_rows = left.shape[0]
    parts = [left.reshape(tok_rows, PAIRS, 128), right.reshape(tok_rows, PAIRS, 128)]
    return jnp.concatenate(parts, axis=-1).reshape(tok_rows, PAIRS * 256)


def unweave(both):
    tok_rows = both.shape[0]
    parts = both.reshape(tok_rows, PAIRS, 2, 128)
    return (
        parts[:, :, 0].reshape(tok_rows, PAIRS * 128),
        parts[:, :, 1].reshape(tok_rows, PAIRS * 128),
    )


def dot(left, right, left_dim, right_dim):
    return lax.dot_general(
        left, right, (((left_dim,), (right_dim,)), ((), ())), preferred_element_type=jnp.float32
    )


def body(
    tokens,
    cotangent,
    block_order,
    w_qkv,
    w_out,
    w_gate,
    w_up,
    w_down,
    attn_gain,
    ffn_gain,
    query_gain,
    key_gain,
):
    tok_rows = tokens.shape[1]
    model_width = tokens.shape[2]
    span_count = lax.axis_size("ctx")
    ways = lax.axis_size("fsdp")
    seq_rows = tok_rows * span_count
    half_rows = tok_rows // 2
    scale = HD ** (-0.5)
    q_width = HEADS * HD
    kv_width = KV_HEADS * HD
    own_rows = w_gate.shape[0]
    hidden_units = w_gate.shape[1]
    part = hidden_units // ways
    low = jnp.bfloat16
    slot_order = block_order.reshape(-1)
    key_spots = (
        slot_order[:, None] * half_rows + jnp.arange(half_rows, dtype=jnp.int32)[None, :]
    ).reshape(-1)
    query_spots = lax.dynamic_slice_in_dim(key_spots, lax.axis_index("ctx") * tok_rows, tok_rows)
    cosines, sines = angles(query_spots)
    key_col = key_spots[:, None]
    query_row = jnp.tile(query_spots, 4)[None, :]

    first_weights = lax.all_gather(
        jnp.concatenate([w_qkv, w_out.T], axis=1), ("ctx", "fsdp"), axis=0, tiled=True
    )
    full_qkv = first_weights[:, : w_qkv.shape[1]]
    out_t = first_weights[:, w_qkv.shape[1] :]
    ffn_own = jnp.concatenate(
        [
            w_gate.reshape(own_rows, ways, part),
            w_up.reshape(own_rows, ways, part),
            w_down.T.reshape(own_rows, ways, part),
        ],
        axis=-1,
    ).transpose(1, 0, 2)
    ffn_rows = exchange(ffn_own, "fsdp", 1)
    cot_low = cotangent.reshape(tok_rows, model_width)
    cot_all = exchange(cot_low, "fsdp", 2, spread=True).reshape(ways * tok_rows, model_width)
    by_head = span_count == KV_HEADS

    tok_f32 = tokens.reshape(tok_rows, model_width).astype(jnp.float32)
    normed, attn_pull = jax.vjp(rms_norm, tok_f32, attn_gain)
    normed_low = normed.astype(low)
    normed_low, cot_all, ffn_rows = lax.optimization_barrier((normed_low, cot_all, ffn_rows))
    ffn_weights = lax.all_gather(
        ffn_rows.reshape(ways * own_rows, 3 * part), "ctx", axis=0, tiled=True
    )
    gate_part = ffn_weights[:, :part]
    up_part = ffn_weights[:, part : 2 * part]
    down_part = ffn_weights[:, 2 * part :]
    projected = jnp.dot(normed_low, full_qkv, preferred_element_type=jnp.float32)
    query_raw = projected[:, :q_width].reshape(tok_rows, HEADS, HD)
    key_raw = projected[:, q_width : q_width + kv_width].reshape(tok_rows, KV_HEADS, HD)
    value_low = projected[:, q_width + kv_width :].astype(low)

    def head_path(raw_heads, gain_row):
        return rotary(rms_norm(raw_heads, gain_row), cosines, sines)

    query_rot, query_pull = jax.vjp(head_path, query_raw, query_gain)
    key_rot, key_pull = jax.vjp(head_path, key_raw, key_gain)
    key_low = key_rot.astype(low).reshape(tok_rows, kv_width)
    query_low = query_rot.astype(low) * low(scale)
    if by_head:
        query_row = jnp.tile(key_spots, 2)[None, :]
        sent = jnp.concatenate(
            [
                query_low.reshape(tok_rows, KV_HEADS, 2 * HD),
                key_low.reshape(tok_rows, KV_HEADS, HD),
                value_low.reshape(tok_rows, KV_HEADS, HD),
            ],
            axis=-1,
        ).transpose(1, 0, 2)
        head_rows = exchange(sent, "ctx", 3).reshape(seq_rows, 4 * HD)
        query_cols = join_heads(head_rows[:, : 2 * HD])
        kv_all = head_rows[:, 2 * HD :]
    else:
        kv_all = lax.all_gather(weave(key_low, value_low), "ctx", axis=0, tiled=True)
        query_cols = head_columns(query_low.reshape(tok_rows, q_width))
    mixed, inverse = attend(query_cols, kv_all, query_row, key_col)
    if by_head:
        attended_low = exchange(split_heads(mixed[0].astype(low), span_count), "ctx", 4)
        attended_low = attended_low.transpose(1, 0, 2).reshape(tok_rows, q_width)
    else:
        attended_low = column_heads(mixed.astype(low), tok_rows)
    hidden = tok_f32 + dot(attended_low, out_t, 1, 1)
    normed_two, ffn_pull = jax.vjp(rms_norm, hidden, ffn_gain)
    two_all = exchange(normed_two.astype(low), "fsdp", 5, spread=True)
    two_all = two_all.reshape(ways * tok_rows, model_width)

    gate_val = dot(two_all, gate_part, 1, 0)
    up_val = dot(two_all, up_part, 1, 0)

    def gated(gate_in, up_in):
        return jax.nn.silu(gate_in) * up_in

    activation, act_pull = jax.vjp(gated, gate_val, up_val)
    act_low = activation.astype(low)
    act_grad = dot(cot_all, down_part, 1, 0)
    gate_grad, up_grad = act_pull(act_grad)
    gate_low = gate_grad.astype(low)
    up_low = up_grad.astype(low)
    grad_ffn = jnp.concatenate(
        [dot(two_all, gate_low, 0, 0), dot(two_all, up_low, 0, 0), dot(cot_all, act_low, 0, 0)],
        axis=1,
    ).astype(low)
    gate_low, up_low, act_low, grad_ffn = lax.optimization_barrier(
        (gate_low, up_low, act_low, grad_ffn)
    )
    grad_ffn = lax.psum_scatter(grad_ffn, "ctx", scatter_dimension=0, tiled=True)
    two_part = dot(gate_low, gate_part, 1, 1) + dot(up_low, up_part, 1, 1)
    two_parts = two_part.astype(low).reshape(ways, tok_rows, model_width)
    normed_two_grad = jnp.sum(exchange(two_parts, "fsdp", 6).astype(jnp.float32), axis=0)

    hidden_back, ffn_gain_grad = ffn_pull(normed_two_grad)
    hidden_grad = cot_low.astype(jnp.float32) + hidden_back
    hidden_low = hidden_grad.astype(low)
    attended_grad = dot(hidden_low, out_t, 1, 0).astype(low)
    if by_head:
        grad_rows = attended_grad.reshape(tok_rows, KV_HEADS, 2 * HD).transpose(1, 0, 2)
        grad_cols = join_heads(exchange(grad_rows, "ctx", 7).reshape(seq_rows, 2 * HD))
    else:
        grad_cols = head_columns(attended_grad)
    query_grad, kv_grad = attend_back(
        query_cols, grad_cols, kv_all, mixed, inverse, query_row, key_col
    )
    if by_head:
        sent = jnp.concatenate(
            [
                split_heads((query_grad[0] * scale).astype(low), span_count),
                kv_grad.reshape(span_count, tok_rows, 2 * HD),
            ],
            axis=-1,
        )
        received = exchange(sent, "ctx", 8).transpose(1, 0, 2)
        query_sum = received[:, :, : 2 * HD].astype(jnp.float32)
        key_sum = received[:, :, 2 * HD : 3 * HD]
        value_sum = received[:, :, 3 * HD :].reshape(tok_rows, kv_width)
    else:
        query_sum = column_heads(query_grad * scale, tok_rows)
        kv_sum = lax.psum_scatter(kv_grad, "ctx", scatter_dimension=0, tiled=True)
        key_sum, value_sum = unweave(kv_sum)

    grad_ffn = lax.all_to_all(
        grad_ffn.reshape(ways, own_rows, 3 * part), "fsdp", 0, 0, tiled=True
    ).transpose(1, 0, 2)
    grad_gate = grad_ffn[:, :, :part].reshape(own_rows, hidden_units).astype(jnp.float32)
    grad_up = grad_ffn[:, :, part : 2 * part].reshape(own_rows, hidden_units).astype(jnp.float32)
    grad_down = grad_ffn[:, :, 2 * part :].reshape(own_rows, hidden_units).T.astype(jnp.float32)

    query_back, query_gain_grad = query_pull(
        query_sum.reshape(tok_rows, HEADS, HD)
    )
    key_back, key_gain_grad = key_pull(
        key_sum.astype(jnp.float32).reshape(tok_rows, KV_HEADS, HD)
    )
    proj_low = jnp.concatenate(
        [
            query_back.reshape(tok_rows, q_width).astype(low),
            key_back.reshape(tok_rows, kv_width).astype(low),
            value_sum,
        ],
        axis=1,
    )
    grad_first = jnp.concatenate(
        [dot(normed_low, proj_low, 0, 0), dot(hidden_low, attended_low, 0, 0)], axis=1
    ).astype(low)
    grad_first, act_low = lax.optimization_barrier((grad_first, act_low))
    block_parts = dot(act_low, down_part, 1, 1).astype(low).reshape(ways, tok_rows, model_width)
    block_sum = jnp.sum(exchange(block_parts, "fsdp", 9).astype(jnp.float32), axis=0)
    block_out = (hidden + block_sum).astype(low)
    grad_first = lax.psum_scatter(
        grad_first, ("ctx", "fsdp"), scatter_dimension=0, tiled=True
    ).astype(jnp.float32)
    grad_qkv = grad_first[:, : w_qkv.shape[1]]
    grad_out = grad_first[:, w_qkv.shape[1] :].T
    normed_grad = dot(proj_low, full_qkv, 1, 1)
    input_back, attn_gain_grad = attn_pull(normed_grad)
    input_grad = (hidden_grad + input_back).astype(low)
    attn_gain_grad, ffn_gain_grad, query_gain_grad, key_gain_grad = lax.psum(
        (attn_gain_grad, ffn_gain_grad, query_gain_grad, key_gain_grad), ("ctx", "fsdp")
    )
    return (
        block_out.reshape(1, tok_rows, model_width),
        input_grad.reshape(1, tok_rows, model_width),
        grad_qkv,
        grad_out,
        grad_gate,
        grad_up,
        grad_down,
        attn_gain_grad,
        ffn_gain_grad,
        query_gain_grad,
        key_gain_grad,
    )


def solution(mesh):
    placed = (
        P("fsdp", "ctx", None),
        P("fsdp", "ctx", None),
        P("fsdp", None),
        P(("ctx", "fsdp"), None),
        P(None, ("ctx", "fsdp")),
        P(("ctx", "fsdp"), None),
        P(("ctx", "fsdp"), None),
        P(None, ("ctx", "fsdp")),
        P(),
        P(),
        P(),
        P(),
    )
    return jax.shard_map(
        body,
        mesh=mesh,
        in_specs=placed,
        out_specs=(
            P("fsdp", "ctx", None),
            P("fsdp", "ctx", None),
            P(("ctx", "fsdp"), None),
            P(None, ("ctx", "fsdp")),
            P(("ctx", "fsdp"), None),
            P(("ctx", "fsdp"), None),
            P(None, ("ctx", "fsdp")),
            P(),
            P(),
            P(),
            P(),
        ),
        check_vma=False,
    )
```

```python
import functools

import jax
import jax.numpy as jnp
from jax import lax
from jax.experimental import pallas as pl
from jax.experimental.pallas import tpu as pltpu
from jax.sharding import PartitionSpec as P

HEADS = 16
KV_HEADS = 8
HD = 64
KBLOCK = 512


EPS = 1e-05
THETA = 1000000.0


def rms_norm(inputs, gain_row):
    return inputs * lax.rsqrt(jnp.mean(inputs * inputs, axis=-1, keepdims=True) + EPS) * gain_row


def rotary(inputs, cosines, sines):
    half_width = inputs.shape[-1] // 2
    turned = jnp.concatenate([-inputs[..., half_width:], inputs[..., :half_width]], axis=-1)
    return inputs * cosines + turned * sines


def angles(positions):
    exponent = jnp.arange(0, HD, 2).astype(jnp.float32) / HD
    inverse = jnp.power(THETA, -exponent)
    phases = positions.astype(jnp.float32)[:, None] * inverse[None, :]
    phases = jnp.concatenate([phases, phases], axis=-1)
    return (jnp.cos(phases)[:, None, :], jnp.sin(phases)[:, None, :])


PAIRS = KV_HEADS // 2
VMEM_LIMIT = 50 * 1024 * 1024


def key_depth(columns):
    return KBLOCK // 2


def forward_kernel(q_ref, kv_ref, qspot_ref, kspot_ref, out_ref, total_ref):
    query_cols = q_ref[0]
    width, columns = query_cols.shape
    depth = key_depth(columns)
    query_spots = qspot_ref[0]

    def step(block, carry):
        mixed, total = carry
        rows = pl.ds(pl.multiple_of(block * depth, depth), depth)
        keys = kv_ref[rows, :width]
        values = kv_ref[rows, width:]
        scores = jnp.dot(keys, query_cols, preferred_element_type=jnp.float32)
        allowed = query_spots >= kspot_ref[rows, :]
        weights = jnp.where(allowed, jnp.exp(scores), 0.0)
        total = total + jnp.sum(weights, axis=0, keepdims=True)
        mixed = mixed + lax.dot_general(
            values,
            weights.astype(jnp.bfloat16),
            (((0,), (0,)), ((), ())),
            preferred_element_type=jnp.float32,
        )
        return mixed, total

    mixed, total = lax.fori_loop(
        0,
        kv_ref.shape[0] // depth,
        step,
        (jnp.zeros((width, columns), jnp.float32), jnp.zeros((1, columns), jnp.float32)),
    )
    out_ref[0] = mixed / total
    total_ref[0] = 1.0 / total


def backward_kernel(shared, q_ref, do_ref, kv_ref, out_ref, inv_ref, qspot_ref, kspot_ref, dq_ref, dkv_ref):
    query_cols = q_ref[0]
    width, columns = query_cols.shape
    depth = key_depth(columns)
    grad_cols = do_ref[0]
    query_spots = qspot_ref[0]
    inverse = inv_ref[0]
    diagonal = jnp.sum(grad_cols.astype(jnp.float32) * out_ref[0], axis=0, keepdims=True)
    last = (((1,), (1,)), ((), ()))
    fresh = pl.program_id(0) == 0 if shared else True

    @pl.when(fresh)
    def _():
        dkv_ref[...] = jnp.zeros_like(dkv_ref)

    def step(block, query_grad):
        rows = pl.ds(pl.multiple_of(block * depth, depth), depth)
        keys = kv_ref[rows, :width]
        values = kv_ref[rows, width:]
        scores = jnp.dot(keys, query_cols, preferred_element_type=jnp.float32)
        allowed = query_spots >= kspot_ref[rows, :]
        probs = jnp.where(allowed, jnp.exp(scores), 0.0) * inverse
        prob_grad = jnp.dot(values, grad_cols, preferred_element_type=jnp.float32)
        score_low = (probs * (prob_grad - diagonal)).astype(jnp.bfloat16)
        dkv_ref[rows, :width] += lax.dot_general(
            score_low, query_cols, last, preferred_element_type=jnp.float32
        )
        dkv_ref[rows, width:] += lax.dot_general(
            probs.astype(jnp.bfloat16), grad_cols, last, preferred_element_type=jnp.float32
        )
        return query_grad + lax.dot_general(
            keys, score_low, (((0,), (0,)), ((), ())), preferred_element_type=jnp.float32
        )

    dq_ref[0] = lax.fori_loop(
        0, kv_ref.shape[0] // depth, step, jnp.zeros(query_cols.shape, jnp.float32)
    )


def head_columns(rows_by_heads):
    tok_rows = rows_by_heads.shape[0]
    cols = rows_by_heads.reshape(tok_rows, PAIRS, 2, 2, HD).transpose(1, 4, 2, 3, 0)
    cols = cols.reshape(PAIRS, HD, 2, 2 * tok_rows)
    empty = jnp.zeros_like(cols[:, :, 0])
    top = jnp.concatenate([cols[:, :, 0], empty], axis=-1)
    low = jnp.concatenate([empty, cols[:, :, 1]], axis=-1)
    return jnp.concatenate([top, low], axis=1)


def column_heads(cols, tok_rows):
    top = cols[:, :HD, : 2 * tok_rows].reshape(PAIRS, HD, 2, tok_rows)
    low = cols[:, HD:, 2 * tok_rows :].reshape(PAIRS, HD, 2, tok_rows)
    both = jnp.stack([top, low], axis=1)
    return both.transpose(4, 0, 1, 3, 2).reshape(tok_rows, HEADS * HD)


def attend(query_cols, kv_all, query_row, key_col):
    seq_rows = kv_all.shape[0]
    groups, width, columns = query_cols.shape
    shared = kv_all.shape[1] == 2 * width
    return pl.pallas_call(
        forward_kernel,
        grid=(groups,),
        in_specs=[
            pl.BlockSpec((1, width, columns), lambda p: (p, 0, 0)),
            pl.BlockSpec((seq_rows, 2 * width), lambda p: (0, 0 if shared else p)),
            pl.BlockSpec((1, 1, columns), lambda p: (p, 0, 0)),
            pl.BlockSpec((seq_rows, 1), lambda p: (0, 0)),
        ],
        out_specs=[
            pl.BlockSpec((1, width, columns), lambda p: (p, 0, 0)),
            pl.BlockSpec((1, 1, columns), lambda p: (p, 0, 0)),
        ],
        out_shape=[
            jax.ShapeDtypeStruct((groups, width, columns), jnp.float32),
            jax.ShapeDtypeStruct((groups, 1, columns), jnp.float32),
        ],
        compiler_params=pltpu.CompilerParams(vmem_limit_bytes=VMEM_LIMIT),
        cost_estimate=pl.CostEstimate(
            flops=4 * groups * width * columns * seq_rows,
            bytes_accessed=12 * 1024 * 1024,
            transcendentals=groups * columns * seq_rows,
        ),
    )(query_cols, kv_all, query_row, key_col)


def attend_back(query_cols, grad_cols, kv_all, mixed, inverse, query_row, key_col):
    seq_rows = kv_all.shape[0]
    groups, width, columns = query_cols.shape
    shared = kv_all.shape[1] == 2 * width
    return pl.pallas_call(
        functools.partial(backward_kernel, shared),
        grid=(groups,),
        in_specs=[
            pl.BlockSpec((1, width, columns), lambda p: (p, 0, 0)),
            pl.BlockSpec((1, width, columns), lambda p: (p, 0, 0)),
            pl.BlockSpec((seq_rows, 2 * width), lambda p: (0, 0 if shared else p)),
            pl.BlockSpec((1, width, columns), lambda p: (p, 0, 0)),
            pl.BlockSpec((1, 1, columns), lambda p: (p, 0, 0)),
            pl.BlockSpec((1, 1, columns), lambda p: (p, 0, 0)),
            pl.BlockSpec((seq_rows, 1), lambda p: (0, 0)),
        ],
        out_specs=[
            pl.BlockSpec((1, width, columns), lambda p: (p, 0, 0)),
            pl.BlockSpec((seq_rows, 2 * width), lambda p: (0, 0 if shared else p)),
        ],
        out_shape=[
            jax.ShapeDtypeStruct((groups, width, columns), jnp.float32),
            jax.ShapeDtypeStruct(kv_all.shape, jnp.float32),
        ],
        compiler_params=pltpu.CompilerParams(vmem_limit_bytes=VMEM_LIMIT),
        cost_estimate=pl.CostEstimate(
            flops=10 * groups * width * columns * seq_rows,
            bytes_accessed=20 * 1024 * 1024,
            transcendentals=groups * columns * seq_rows,
        ),
    )(query_cols, grad_cols, kv_all, mixed, inverse, query_row, key_col)


def exchange_kernel(axis, count, spread, src, dst, own_sem, send_sems, recv_sems):
    me = lax.axis_index(axis)
    barrier = pltpu.get_barrier_semaphore()
    for step in range(1, count):
        pl.semaphore_signal(
            barrier,
            inc=1,
            device_id={axis: lax.rem(me + step, count)},
            device_id_type=pl.DeviceIdType.MESH,
        )
    pl.semaphore_wait(barrier, count - 1)
    copies = []
    for step in range(1, count):
        peer = lax.rem(me + step, count)
        copies.append(
            pltpu.make_async_remote_copy(
                src_ref=src if spread else src.at[peer],
                dst_ref=dst.at[me],
                send_sem=send_sems.at[step - 1],
                recv_sem=recv_sems.at[step - 1],
                device_id={axis: peer},
                device_id_type=pl.DeviceIdType.MESH,
            )
        )
    for copy in copies:
        copy.start()
    own = pltpu.make_async_copy(src if spread else src.at[me], dst.at[me], own_sem)
    own.start()
    own.wait()
    for copy in copies:
        copy.wait()


def exchange(block, axis, number, spread=False):
    count = lax.axis_size(axis)
    shape = (count,) + (block.shape if spread else block.shape[1:])
    return pl.pallas_call(
        functools.partial(exchange_kernel, axis, count, spread),
        in_specs=[pl.BlockSpec(memory_space=pl.ANY)],
        out_specs=pl.BlockSpec(memory_space=pl.ANY),
        out_shape=jax.ShapeDtypeStruct(shape, block.dtype),
        scratch_shapes=[
            pltpu.SemaphoreType.DMA,
            pltpu.SemaphoreType.DMA((count - 1,)),
            pltpu.SemaphoreType.DMA((count - 1,)),
        ],
        compiler_params=pltpu.CompilerParams(collective_id=number, has_side_effects=True),
        cost_estimate=pl.CostEstimate(flops=0, bytes_accessed=40_000_000, transcendentals=0),
    )(block)


def split_heads(cols, spans):
    chunks, _, columns = cols.shape
    rows = cols.reshape(chunks, HD, 2, columns // 2).transpose(0, 3, 2, 1)
    return rows.reshape(spans, chunks * columns // (2 * spans), 2 * HD)


def join_heads(rows):
    chunks = rows.shape[0] // KBLOCK
    return rows.reshape(chunks, KBLOCK, 2, HD).transpose(0, 3, 2, 1).reshape(chunks, HD, 2 * KBLOCK)


def weave(left, right):
    tok_rows = left.shape[0]
    parts = [left.reshape(tok_rows, PAIRS, 128), right.reshape(tok_rows, PAIRS, 128)]
    return jnp.concatenate(parts, axis=-1).reshape(tok_rows, PAIRS * 256)


def unweave(both):
    tok_rows = both.shape[0]
    parts = both.reshape(tok_rows, PAIRS, 2, 128)
    return (
        parts[:, :, 0].reshape(tok_rows, PAIRS * 128),
        parts[:, :, 1].reshape(tok_rows, PAIRS * 128),
    )


def dot(left, right, left_dim, right_dim):
    return lax.dot_general(
        left, right, (((left_dim,), (right_dim,)), ((), ())), preferred_element_type=jnp.float32
    )


def body(
    tokens,
    cotangent,
    block_order,
    w_qkv,
    w_out,
    w_gate,
    w_up,
    w_down,
    attn_gain,
    ffn_gain,
    query_gain,
    key_gain,
):
    tok_rows = tokens.shape[1]
    model_width = tokens.shape[2]
    span_count = lax.axis_size("ctx")
    ways = lax.axis_size("fsdp")
    seq_rows = tok_rows * span_count
    half_rows = tok_rows // 2
    scale = HD ** (-0.5)
    q_width = HEADS * HD
    kv_width = KV_HEADS * HD
    own_rows = w_gate.shape[0]
    hidden_units = w_gate.shape[1]
    part = hidden_units // ways
    low = jnp.bfloat16
    slot_order = block_order.reshape(-1)
    key_spots = (
        slot_order[:, None] * half_rows + jnp.arange(half_rows, dtype=jnp.int32)[None, :]
    ).reshape(-1)
    query_spots = lax.dynamic_slice_in_dim(key_spots, lax.axis_index("ctx") * tok_rows, tok_rows)
    cosines, sines = angles(query_spots)
    key_col = key_spots[:, None]
    query_row = jnp.tile(query_spots, 4 * PAIRS).reshape(PAIRS, 1, 4 * tok_rows)

    first_weights = lax.all_gather(
        jnp.concatenate([w_qkv, w_out.T], axis=1), ("ctx", "fsdp"), axis=0, tiled=True
    )
    full_qkv = first_weights[:, : w_qkv.shape[1]]
    out_t = first_weights[:, w_qkv.shape[1] :]
    ffn_own = jnp.concatenate(
        [
            w_gate.reshape(own_rows, ways, part),
            w_up.reshape(own_rows, ways, part),
            w_down.T.reshape(own_rows, ways, part),
        ],
        axis=-1,
    ).transpose(1, 0, 2)
    ffn_rows = exchange(ffn_own, "fsdp", 1)
    cot_low = cotangent.reshape(tok_rows, model_width)
    cot_all = exchange(cot_low, "fsdp", 2, spread=True).reshape(ways * tok_rows, model_width)
    by_head = span_count == KV_HEADS

    tok_f32 = tokens.reshape(tok_rows, model_width).astype(jnp.float32)
    normed, attn_pull = jax.vjp(rms_norm, tok_f32, attn_gain)
    normed_low = normed.astype(low)
    normed_low, cot_all, ffn_rows, cosines, sines = lax.optimization_barrier(
        (normed_low, cot_all, ffn_rows, cosines, sines)
    )
    ffn_weights = lax.all_gather(
        ffn_rows.reshape(ways * own_rows, 3 * part), "ctx", axis=0, tiled=True
    )
    gate_part = ffn_weights[:, :part]
    up_part = ffn_weights[:, part : 2 * part]
    down_part = ffn_weights[:, 2 * part :]
    projected = jnp.dot(normed_low, full_qkv, preferred_element_type=jnp.float32)
    query_raw = projected[:, :q_width].reshape(tok_rows, HEADS, HD)
    key_raw = projected[:, q_width : q_width + kv_width].reshape(tok_rows, KV_HEADS, HD)
    value_low = projected[:, q_width + kv_width :].astype(low)

    def head_path(raw_heads, gain_row):
        return rotary(rms_norm(raw_heads, gain_row), cosines, sines)

    query_rot, query_pull = jax.vjp(head_path, query_raw, query_gain)
    key_rot, key_pull = jax.vjp(head_path, key_raw, key_gain)
    key_low = key_rot.astype(low).reshape(tok_rows, kv_width)
    query_low = query_rot.astype(low) * low(scale)
    if by_head:
        query_row = jnp.tile(key_spots.reshape(-1, 1, KBLOCK), (1, 1, 2))
        sent = jnp.concatenate(
            [
                query_low.reshape(tok_rows, KV_HEADS, 2 * HD),
                key_low.reshape(tok_rows, KV_HEADS, HD),
                value_low.reshape(tok_rows, KV_HEADS, HD),
            ],
            axis=-1,
        ).transpose(1, 0, 2)
        head_rows = exchange(sent, "ctx", 3).reshape(seq_rows, 4 * HD)
        query_cols = join_heads(head_rows[:, : 2 * HD])
        kv_all = head_rows[:, 2 * HD :]
    else:
        kv_all = lax.all_gather(weave(key_low, value_low), "ctx", axis=0, tiled=True)
        query_cols = head_columns(query_low.reshape(tok_rows, q_width))
    mixed, inverse = attend(query_cols, kv_all, query_row, key_col)
    if by_head:
        attended_low = exchange(split_heads(mixed.astype(low), span_count), "ctx", 4)
        attended_low = attended_low.transpose(1, 0, 2).reshape(tok_rows, q_width)
    else:
        attended_low = column_heads(mixed.astype(low), tok_rows)
    hidden = tok_f32 + dot(attended_low, out_t, 1, 1)
    normed_two, ffn_pull = jax.vjp(rms_norm, hidden, ffn_gain)
    two_all = exchange(normed_two.astype(low), "fsdp", 5, spread=True)
    two_all = two_all.reshape(ways * tok_rows, model_width)

    gate_val = dot(two_all, gate_part, 1, 0)
    up_val = dot(two_all, up_part, 1, 0)

    def gated(gate_in, up_in):
        return jax.nn.silu(gate_in) * up_in

    activation, act_pull = jax.vjp(gated, gate_val, up_val)
    act_low = activation.astype(low)
    act_grad = dot(cot_all, down_part, 1, 0)
    gate_grad, up_grad = act_pull(act_grad)
    gate_low = gate_grad.astype(low)
    up_low = up_grad.astype(low)
    grad_ffn = jnp.concatenate(
        [dot(two_all, gate_low, 0, 0), dot(two_all, up_low, 0, 0), dot(cot_all, act_low, 0, 0)],
        axis=1,
    ).astype(low)
    gate_low, up_low, act_low, grad_ffn = lax.optimization_barrier(
        (gate_low, up_low, act_low, grad_ffn)
    )
    grad_ffn = lax.psum_scatter(grad_ffn, "ctx", scatter_dimension=0, tiled=True)
    two_part = dot(gate_low, gate_part, 1, 1) + dot(up_low, up_part, 1, 1)
    two_parts = two_part.astype(low).reshape(ways, tok_rows, model_width)
    normed_two_grad = jnp.sum(exchange(two_parts, "fsdp", 6).astype(jnp.float32), axis=0)

    hidden_back, ffn_gain_grad = ffn_pull(normed_two_grad)
    hidden_grad = cot_low.astype(jnp.float32) + hidden_back
    hidden_low = hidden_grad.astype(low)
    attended_grad = dot(hidden_low, out_t, 1, 0).astype(low)
    if by_head:
        grad_rows = attended_grad.reshape(tok_rows, KV_HEADS, 2 * HD).transpose(1, 0, 2)
        grad_cols = join_heads(exchange(grad_rows, "ctx", 7).reshape(seq_rows, 2 * HD))
    else:
        grad_cols = head_columns(attended_grad)
    query_grad, kv_grad = attend_back(
        query_cols, grad_cols, kv_all, mixed, inverse, query_row, key_col
    )
    if by_head:
        sent = jnp.concatenate(
            [
                split_heads((query_grad * scale).astype(low), span_count),
                kv_grad.astype(low).reshape(span_count, tok_rows, 2 * HD),
            ],
            axis=-1,
        )
        received = exchange(sent, "ctx", 8).transpose(1, 0, 2)
        query_sum = received[:, :, : 2 * HD].astype(jnp.float32)
        key_sum = received[:, :, 2 * HD : 3 * HD]
        value_sum = received[:, :, 3 * HD :].reshape(tok_rows, kv_width)
    else:
        query_sum = column_heads(query_grad * scale, tok_rows)
        kv_sum = lax.psum_scatter(kv_grad.astype(low), "ctx", scatter_dimension=0, tiled=True)
        key_sum, value_sum = unweave(kv_sum)

    grad_ffn = lax.all_to_all(
        grad_ffn.reshape(ways, own_rows, 3 * part), "fsdp", 0, 0, tiled=True
    ).transpose(1, 0, 2)
    grad_gate = grad_ffn[:, :, :part].reshape(own_rows, hidden_units).astype(jnp.float32)
    grad_up = grad_ffn[:, :, part : 2 * part].reshape(own_rows, hidden_units).astype(jnp.float32)
    grad_down = grad_ffn[:, :, 2 * part :].reshape(own_rows, hidden_units).T.astype(jnp.float32)

    query_back, query_gain_grad = query_pull(
        query_sum.reshape(tok_rows, HEADS, HD)
    )
    key_back, key_gain_grad = key_pull(
        key_sum.astype(jnp.float32).reshape(tok_rows, KV_HEADS, HD)
    )
    proj_low = jnp.concatenate(
        [
            query_back.reshape(tok_rows, q_width).astype(low),
            key_back.reshape(tok_rows, kv_width).astype(low),
            value_sum,
        ],
        axis=1,
    )
    grad_first = jnp.concatenate(
        [dot(normed_low, proj_low, 0, 0), dot(hidden_low, attended_low, 0, 0)], axis=1
    ).astype(low)
    grad_first, act_low = lax.optimization_barrier((grad_first, act_low))
    block_parts = dot(act_low, down_part, 1, 1).astype(low).reshape(ways, tok_rows, model_width)
    block_sum = jnp.sum(exchange(block_parts, "fsdp", 9).astype(jnp.float32), axis=0)
    block_out = (hidden + block_sum).astype(low)
    grad_first = lax.psum_scatter(
        grad_first, ("ctx", "fsdp"), scatter_dimension=0, tiled=True
    ).astype(jnp.float32)
    grad_qkv = grad_first[:, : w_qkv.shape[1]]
    grad_out = grad_first[:, w_qkv.shape[1] :].T
    normed_grad = dot(proj_low, full_qkv, 1, 1)
    input_back, attn_gain_grad = attn_pull(normed_grad)
    input_grad = (hidden_grad + input_back).astype(low)
    attn_gain_grad, ffn_gain_grad, query_gain_grad, key_gain_grad = lax.psum(
        (attn_gain_grad, ffn_gain_grad, query_gain_grad, key_gain_grad), ("ctx", "fsdp")
    )
    return (
        block_out.reshape(1, tok_rows, model_width),
        input_grad.reshape(1, tok_rows, model_width),
        grad_qkv,
        grad_out,
        grad_gate,
        grad_up,
        grad_down,
        attn_gain_grad,
        ffn_gain_grad,
        query_gain_grad,
        key_gain_grad,
    )


def solution(mesh):
    placed = (
        P("fsdp", "ctx", None),
        P("fsdp", "ctx", None),
        P("fsdp", None),
        P(("ctx", "fsdp"), None),
        P(None, ("ctx", "fsdp")),
        P(("ctx", "fsdp"), None),
        P(("ctx", "fsdp"), None),
        P(None, ("ctx", "fsdp")),
        P(),
        P(),
        P(),
        P(),
    )
    return jax.shard_map(
        body,
        mesh=mesh,
        in_specs=placed,
        out_specs=(
            P("fsdp", "ctx", None),
            P("fsdp", "ctx", None),
            P(("ctx", "fsdp"), None),
            P(None, ("ctx", "fsdp")),
            P(("ctx", "fsdp"), None),
            P(("ctx", "fsdp"), None),
            P(None, ("ctx", "fsdp")),
            P(),
            P(),
            P(),
            P(),
        ),
        check_vma=False,
    )
```
